256 devices in a mesh: row: 32 (over z_lo, y, core), col: 8 (over z_hi, x).
Axes of the slice: x: 4, y: 4, z: 8 (z_hi: 2, z_lo: 4; z = z_hi * 4 + z_lo), core: 2. Of those that a mesh axis runs over, the one named last changes fastest.
Arguments:
- weights: bfloat16 [8192, 32768], P('row', 'col'), may hold values from -6 to 6
- panel_first: float32 [256, 32768], P('row', 'col'), may hold values from -1 to 2, as said below
- panel_second: float32 [256, 32768], P('row', 'col'), may hold values from -1 to 2, as said below
- removed_first: int32 [512], P('col'), may hold values from -1 to 4095, as said below
- removed_second: int32 [512], P('col'), may hold values from -1 to 4095, as said below
Outputs:
- pruned: bfloat16 [8192, 32768], P('row', 'col')
The draws below stay inside these ranges and needn't reach their ends.
Inputs may be any that keep to these rules, and one draw needn't show every extreme that they name: `removed_first`: in each list every owner's live slots come first; there are 256 live slots in all, at most 64 for one owner and exactly 64 for some owner; live values of one owner are distinct, and the two lists name no column twice. `removed_second`: same form as removed_first, with its own owners. `panel_first`: together with panel_second, its entries at the columns S1 and S2 are the rows of one symmetric positive definite matrix of order 2 * 256. `panel_second`: rows of the same inverse Hessian as panel_first, for the columns S2.
All inputs are finite; a program needn't handle non-finite values.
Results may differ from the reference program's by a relative error of at most 0.001.
Values may be sent and summed in bfloat16 or wider, within the bound.
No kernel may reach another device: no remote copies, remote signals or barrier semaphores. Data moves between devices by JAX's collectives and lax.ppermute only.
A program may use at most 64 MiB of HBM per device.

```python
import jax
import jax.numpy as jnp
from jax import lax

ROWS = 8192
COLS = 32768
K = 256
CDEV = 4096
OWNERS = 8
SLOTS = 64
N_COL = 8


def removed_lists(key):
    results = []
    owner_keys = jax.random.split(jax.random.fold_in(key, 7), OWNERS)
    orders = jax.vmap(lambda okey: jax.random.permutation(okey, CDEV))(owner_keys)
    for list_index in range(2):
        list_key = jax.random.fold_in(key, 11 + list_index)
        busiest = jax.random.randint(jax.random.fold_in(list_key, 1), (), 0, OWNERS)
        spare = K - SLOTS
        others = (OWNERS - 1) * SLOTS
        shuffled = jax.random.permutation(jax.random.fold_in(list_key, 2), others)
        chosen = jnp.zeros((others,), jnp.int32).at[shuffled[:spare]].set(1)
        rest = chosen.reshape(OWNERS - 1, SLOTS).sum(1)
        owner = jnp.arange(OWNERS, dtype=jnp.int32)
        rest_index = jnp.clip(owner - (owner > busiest).astype(jnp.int32), 0, OWNERS - 2)
        counts = jnp.where(owner == busiest, SLOTS, rest[rest_index])
        slot_ids = jnp.arange(SLOTS, dtype=jnp.int32)
        picked = orders[:, list_index * SLOTS:(list_index + 1) * SLOTS]
        filled = jnp.where(slot_ids[None, :] < counts[:, None], picked, -1)
        results.append(filled.reshape(-1).astype(jnp.int32))
    return results


def compact_columns(removed):
    present = removed >= 0
    owner = (jnp.arange(removed.shape[0]) // SLOTS).astype(jnp.int32)
    global_col = owner * CDEV + jnp.where(present, removed, 0).astype(jnp.int32)
    position = jnp.cumsum(present.astype(jnp.int32)) - 1
    target = jnp.where(present, position, K).astype(jnp.int32)
    return jnp.zeros((K,), jnp.int32).at[target].set(global_col, mode='drop')


def panel_pair(key):
    first_list, second_list = removed_lists(key)
    cols_first = compact_columns(first_list)
    cols_second = compact_columns(second_list)
    gkey = jax.random.fold_in(key, 21)
    sigma = 0.3 / (2.0 * K) ** 0.5
    raw = jax.random.normal(jax.random.fold_in(gkey, 1), (2 * K, 2 * K), jnp.float32) * sigma
    base = jnp.clip(jax.random.normal(jax.random.fold_in(gkey, 2), (2, K, COLS), jnp.float32), -4.0, 4.0) / K ** 0.5
    off_part = (raw + raw.T) / 2.0 ** 0.5
    off_part = off_part * (1.0 - jnp.eye(2 * K, dtype=jnp.float32))
    diag_part = jax.random.uniform(jax.random.fold_in(gkey, 4), (2 * K,), jnp.float32, 1.2, 2.0)
    block = off_part + jnp.diag(diag_part)
    first = base[0].at[:, cols_first].set(block[:K, :K]).at[:, cols_second].set(block[:K, K:])
    second = base[1].at[:, cols_first].set(block[K:, :K]).at[:, cols_second].set(block[K:, K:])
    return (first, second)


def draw_panel_first(key, part):
    return panel_pair(key)[0]


def draw_panel_second(key, part):
    return panel_pair(key)[1]


def draw_removed_first(key, part):
    return removed_lists(key)[0]


def draw_removed_second(key, part):
    return removed_lists(key)[1]


def block_scale(stream_key, dims, cuts, least, largest):
    def one(axis_at, shards_of):
        heights = jax.random.uniform(jax.random.fold_in(jax.random.fold_in(stream_key, 6), axis_at), (shards_of,), jnp.float32, least / len(cuts), largest / len(cuts))
        return jnp.repeat(jnp.exp(heights), dims[axis_at] // shards_of).reshape((-1,) + (1,) * (len(dims) - axis_at - 1))

    gain = one(*cuts[0])
    for cut in cuts[1:]:
        gain = gain * one(*cut)
    return gain


def centred(stream_key, shape, spread, most, shards=(), kind=jnp.bfloat16):
    loudness = block_scale(stream_key, shape, shards, -0.22, 0.18) if shards else 1.0
    drawn = jax.random.normal(stream_key, shape, jnp.float32) * spread * loudness
    return jnp.minimum(jnp.maximum(drawn, -most), most).astype(kind)


def setup_inputs(seed: int = 0) -> dict:
    seeds = jax.random.split(jax.random.key(seed), 6)
    weights = centred(seeds[0], (ROWS, COLS), 1.0, 6.0, ((0, 32), (1, 8)))
    panel_first = draw_panel_first(jax.random.fold_in(seeds[5], 71), 0)
    panel_second = draw_panel_second(jax.random.fold_in(seeds[5], 71), 0)
    removed_first = draw_removed_first(jax.random.fold_in(seeds[5], 71), 0)
    removed_second = draw_removed_second(jax.random.fold_in(seeds[5], 71), 0)
    return dict(weights=weights, panel_first=panel_first, panel_second=panel_second, removed_first=removed_first, removed_second=removed_second)


highest = lax.Precision.HIGHEST

def compact(removed):
    present = removed >= 0
    owner = (jnp.arange(removed.shape[0]) // SLOTS).astype(jnp.int32)
    global_col = owner * CDEV + jnp.where(present, removed, 0).astype(jnp.int32)
    position = jnp.cumsum(present.astype(jnp.int32)) - 1
    target = jnp.where(present, position, K).astype(jnp.int32)
    return jnp.zeros((K,), jnp.int32).at[target].set(global_col.astype(jnp.int32), mode='drop')

def apply_inverse(factor, matrix):
    return jax.scipy.linalg.cho_solve((factor, True), matrix.T).T

def reference(weights, panel_first, panel_second, removed_first, removed_second):
    cols_first = compact(removed_first)
    cols_second = compact(removed_second)
    factor_first = jnp.linalg.cholesky(panel_first[:, cols_first])
    coef_first = apply_inverse(factor_first, weights[:, cols_first].astype(jnp.float32))
    coupling = apply_inverse(factor_first, panel_second[:, cols_first])
    h_second = panel_second[:, cols_second] - jnp.dot(coupling, panel_first[:, cols_second], precision=highest)
    factor_second = jnp.linalg.cholesky(h_second)
    w1_second = weights[:, cols_second].astype(jnp.float32) - jnp.dot(coef_first, panel_first[:, cols_second], precision=highest)
    coef_second = apply_inverse(factor_second, w1_second)

    def one_block(index):
        start = (index * CDEV).astype(jnp.int32)
        w_block = lax.dynamic_slice_in_dim(weights, start, CDEV, 1).astype(jnp.float32)
        first_block = lax.dynamic_slice_in_dim(panel_first, start, CDEV, 1)
        second_block = lax.dynamic_slice_in_dim(panel_second, start, CDEV, 1)
        updated = w_block - jnp.dot(coef_first, first_block, precision=highest)
        downdated = second_block - jnp.dot(coupling, first_block, precision=highest)
        return (updated - jnp.dot(coef_second, downdated, precision=highest)).astype(jnp.bfloat16)
    blocks = lax.map(one_block, jnp.arange(N_COL, dtype=jnp.int32))
    return jnp.transpose(blocks, (1, 0, 2)).reshape(ROWS, COLS)
```

```python
import jax
import jax.numpy as jnp
from jax import lax
from jax.experimental import pallas as pl
from jax.experimental.pallas import tpu as pltpu
from jax.sharding import PartitionSpec as P

f32 = jnp.float32
bf16 = jnp.bfloat16
VMEM = pltpu.VMEM
TOLERANCE = 3e-5
DOUBLINGS = 6


def vmem_spec():
    return pl.BlockSpec(memory_space=VMEM)


def halves(value):
    high = value.astype(bf16)
    low = (value - high.astype(f32)).astype(bf16)
    return high, low


def dot(a, b):
    return jnp.dot(a, b, preferred_element_type=f32)


def product(a, b):
    a_high, a_low = halves(a)
    b_high, b_low = halves(b)
    return dot(a_high, b_high) + (dot(a_high, b_low) + dot(a_low, b_high))


def extract_kernel(weights_ref, panels_ref, chosen_ref, out_ref, acc):
    step = pl.program_id(0)
    tile = weights_ref.shape[1]
    rows = weights_ref.shape[0]
    height = panels_ref.shape[0]

    @pl.when(step == 0)
    def _():
        acc[...] = jnp.zeros_like(acc)

    chosen = chosen_ref[...]
    column = lax.broadcasted_iota(jnp.int32, (tile, chosen.shape[1]), 0) + step * tile
    onehot = (column == chosen).astype(f32).astype(bf16)
    panels = panels_ref[...]
    high = panels.astype(bf16)
    rest = panels - high.astype(f32)
    middle = rest.astype(bf16)
    low = (rest - middle.astype(f32)).astype(bf16)
    acc[0:rows, :] += dot(weights_ref[...], onehot)
    acc[rows : rows + 3 * height, :] += dot(jnp.concatenate([high, middle, low], axis=0), onehot)

    @pl.when(step == pl.num_programs(0) - 1)
    def _():
        acc[rows + 3 * height :, :] = jnp.broadcast_to(
            (chosen >= 0).astype(f32), (height, chosen.shape[1])
        )
        out_ref[...] = acc[...].astype(bf16)


def extract(weights, panels, chosen):
    rows, width = weights.shape
    height = panels.shape[0]
    tile = 1024
    slots = chosen.shape[1]
    total = rows + 4 * height
    return pl.pallas_call(
        extract_kernel,
        out_shape=jax.ShapeDtypeStruct((total, slots), bf16),
        grid=(width // tile,),
        in_specs=[
            pl.BlockSpec((rows, tile), lambda i: (0, i)),
            pl.BlockSpec((height, tile), lambda i: (0, i)),
            pl.BlockSpec((1, slots), lambda i: (0, 0)),
        ],
        out_specs=pl.BlockSpec((total, slots), lambda i: (0, 0)),
        scratch_shapes=[VMEM((total, slots), f32)],
        name="extract",
    )(weights, panels, chosen)


def compact_kernel(slots_ref, columns_ref, entries_ref, acc):
    owners, total, slots = slots_ref.shape
    order = entries_ref.shape[1]
    height = entries_ref.shape[0]
    rows = columns_ref.shape[0]
    half = slots // 2
    lane = lax.broadcasted_iota(jnp.int32, (1, slots), 1)
    in_second = lane >= half
    slot = jnp.where(in_second, lane - half, lane)
    target = lax.broadcasted_iota(jnp.int32, (order, slots), 0)
    per_list = order // 2
    per_device = height // 2
    base_first = jnp.zeros((1, 1), f32)
    base_second = jnp.zeros((1, 1), f32)
    for owner in range(owners):
        live = slots_ref[owner, total - height : total, :].astype(f32)[0:1, :]
        start = jnp.where(in_second, base_second, base_first).astype(jnp.int32)
        position = start + slot
        place = (
            (position // per_device) * height
            + jnp.where(in_second, per_device, 0)
            + position % per_device
        )
        place = jnp.where(live > 0.5, place, -1)
        move = (target == place).astype(f32).astype(bf16)
        share = lax.dot_general(
            slots_ref[owner, 0 : total - height, :],
            move,
            (((1,), (1,)), ((), ())),
            preferred_element_type=f32,
        )
        if owner == 0:
            acc[...] = share
        else:
            acc[...] += share
        base_first = base_first + jnp.sum(jnp.where(in_second, 0.0, live), axis=1, keepdims=True)
        base_second = base_second + jnp.sum(jnp.where(in_second, live, 0.0), axis=1, keepdims=True)
    columns_ref[...] = acc[0:rows, :].astype(bf16)
    high = acc[rows : rows + height, :]
    middle = acc[rows + height : rows + 2 * height, :]
    low = acc[rows + 2 * height : rows + 3 * height, :]
    entries_ref[...] = high + (middle + low)


def compact(received, rows, height, order):
    return pl.pallas_call(
        compact_kernel,
        out_shape=(
            jax.ShapeDtypeStruct((rows, order), bf16),
            jax.ShapeDtypeStruct((height, order), f32),
        ),
        in_specs=[vmem_spec()],
        out_specs=(vmem_spec(), vmem_spec()),
        scratch_shapes=[VMEM((rows + 3 * height, order), f32)],
        name="compact",
    )(received)


def solve_kernel(entries_ref, columns_ref, high_ref, low_ref, stacked, inverse):
    order = entries_ref.shape[0]
    rows = columns_ref.shape[0]
    row = lax.broadcasted_iota(jnp.int32, (order, order), 0)
    col = lax.broadcasted_iota(jnp.int32, (order, order), 1)
    entries = entries_ref[...]
    diagonal = jnp.where(row == col, entries, 0.0)
    scale_row = lax.rsqrt(jnp.sum(diagonal, axis=0, keepdims=True))
    scale_col = lax.rsqrt(jnp.sum(diagonal, axis=1, keepdims=True))
    unit = entries * scale_col * scale_row
    rest = jnp.where(row == col, 1.0 - unit, -unit)
    stacked[0:rows, :] = columns_ref[...].astype(f32) * scale_row
    stacked[rows:, :] = rest

    def bound():
        power = stacked[rows:, :]
        return jnp.sum(power * power)

    def going(state):
        count, left = state
        return jnp.logical_and(count < DOUBLINGS, jnp.logical_not(left < TOLERANCE))

    def double(state):
        count, _ = state
        power = stacked[rows:, :]
        result = product(stacked[...], power)
        stacked[0:rows, :] += result[0:rows, :]
        stacked[rows:, :] = result[rows:, :]
        return count + 1, bound()

    _, left = lax.while_loop(going, double, (jnp.int32(0), bound()))
    settled = left < TOLERANCE

    @pl.when(settled)
    def _():
        solved = stacked[0:rows, :]
        solved = (solved + product(solved, stacked[rows:, :])) * scale_row
        high, low = halves(solved)
        high_ref[...] = high
        low_ref[...] = low

    @pl.when(jnp.logical_not(settled))
    def _():
        inverse[...] = entries_ref[...] * scale_col * scale_row

        def pivot(k, carry):
            lanes = lax.broadcasted_iota(jnp.int32, (1, order), 1)
            pivot_row = inverse[pl.ds(k, 1), :]
            head = jnp.sum(jnp.where(lanes == k, pivot_row, 0.0), axis=1, keepdims=True)
            pivot_row = jnp.where(lanes == k, 1.0, pivot_row) / head
            everything = inverse[...]
            column = jnp.sum(jnp.where(col == k, everything, 0.0), axis=1, keepdims=True)
            kept = jnp.where(col == k, 0.0, everything)
            inverse[...] = kept - column * pivot_row
            inverse[pl.ds(k, 1), :] = pivot_row
            return carry

        lax.fori_loop(0, order, pivot, 0)
        whole = entries_ref[...] * scale_col * scale_row
        wanted = columns_ref[...].astype(f32) * scale_row

        def exact(a, b):
            return jnp.dot(a, b, precision=lax.Precision.HIGHEST, preferred_element_type=f32)

        solved = exact(wanted, inverse[...])
        solved = solved + exact(wanted - exact(solved, whole), inverse[...])
        high, low = halves(solved * scale_row)
        high_ref[...] = high
        low_ref[...] = low


def solve(entries, columns):
    rows, order = columns.shape
    return pl.pallas_call(
        solve_kernel,
        out_shape=(jax.ShapeDtypeStruct((rows, order), bf16),) * 2,
        in_specs=[vmem_spec(), vmem_spec()],
        out_specs=(vmem_spec(), vmem_spec()),
        scratch_shapes=[VMEM((rows + order, order), f32), VMEM((order, order), f32)],
        name="solve",
    )(entries, columns)


def update_kernel(weights_ref, panels_ref, high_ref, low_ref, out_ref):
    panel_high, panel_low = halves(panels_ref[...])
    high = high_ref[...]
    change = dot(high, panel_high) + (dot(high, panel_low) + dot(low_ref[...], panel_high))
    out_ref[...] = (weights_ref[...].astype(f32) - change).astype(bf16)


def update(weights, panels, high, low):
    rows, width = weights.shape
    order = panels.shape[0]
    tile = 512
    return pl.pallas_call(
        update_kernel,
        out_shape=jax.ShapeDtypeStruct((rows, width), bf16),
        grid=(width // tile,),
        in_specs=[
            pl.BlockSpec((rows, tile), lambda i: (0, i)),
            pl.BlockSpec((order, tile), lambda i: (0, i)),
            pl.BlockSpec((rows, order), lambda i: (0, 0)),
            pl.BlockSpec((rows, order), lambda i: (0, 0)),
        ],
        out_specs=pl.BlockSpec((rows, tile), lambda i: (0, i)),
        name="update",
    )(weights, panels, high, low)


def on_device(weights, panel_first, panel_second, removed_first, removed_second):
    rows = weights.shape[0]
    row_devices = lax.axis_size("row")
    col_devices = lax.axis_size("col")
    panels = jnp.concatenate([panel_first, panel_second], axis=0)
    height = panels.shape[0]
    order = height * row_devices
    panels_whole = lax.all_gather(panels, "row", axis=0, tiled=True)
    chosen = jnp.concatenate([removed_first, removed_second])[None, :]
    mine = extract(weights, panels, chosen)
    spread = jnp.broadcast_to(mine[None], (col_devices,) + mine.shape)
    received = lax.all_to_all(spread, "col", 0, 0)
    columns, entries = compact(received, rows, height, order)
    entries = jnp.broadcast_to(entries[None], (row_devices,) + entries.shape)
    entries = lax.all_to_all(entries, "row", 0, 0).reshape(order, order)
    high, low = solve(entries, columns)
    return update(weights, panels_whole, high, low)


def solution(mesh):
    return jax.shard_map(
        on_device,
        mesh=mesh,
        in_specs=(P("row", "col"), P("row", "col"), P("row", "col"), P("col"), P("col")),
        out_specs=P("row", "col"),
        check_vma=False,
    )
```

```python
import jax
import jax.numpy as jnp
from jax import lax
from jax.experimental import pallas as pl
from jax.experimental.pallas import tpu as pltpu
from jax.sharding import PartitionSpec as P

f32 = jnp.float32
bf16 = jnp.bfloat16
VMEM = pltpu.VMEM
TOLERANCE = 3e-5
DOUBLINGS = 6
CODE_TOP = 32767.0
CORE, Y_ONE, Y_THREE, Z_ONE, Z_TWO, Z_THREE = 1, 2, 6, 8, 16, 24
X_ONE, X_THREE, Z_HALF = 1, 3, 4
OWNER_ORDER = (0, 4, 1, 5, 3, 7, 2, 6)
ENTRY_ORDER = tuple(c + y * 2 + z * 8 for c in (0, 1) for y in (0, 1, 3, 2) for z in range(4))
PANEL_ORDER = tuple(
    c + y * 2 + z * 8
    for c in (0, 1)
    for ys, zs in (((0, 1), (0, 1)), ((3, 2), (0, 1)), ((0, 3), (2, 3)), ((1, 2), (2, 3)))
    for y in ys
    for z in zs
)


def vmem_spec():
    return pl.BlockSpec(memory_space=VMEM)


def halves(value):
    high = value.astype(bf16)
    low = (value - high.astype(f32)).astype(bf16)
    return high, low


def dot(a, b):
    return jnp.dot(a, b, preferred_element_type=f32)


def product(a, b):
    a_high, a_low = halves(a)
    b_high, b_low = halves(b)
    return dot(a_high, b_high) + (dot(a_high, b_low) + dot(a_low, b_high))


def code_scale(exponent):
    return jnp.exp2(exponent.astype(f32) * 0.125)


def prepare_kernel(first_ref, second_ref, chosen_first_ref, chosen_second_ref, codes_ref, slots_ref):
    panels = jnp.concatenate([first_ref[...], second_ref[...]], axis=0)
    height, width = panels.shape
    size = jnp.abs(panels)
    most = jnp.maximum(jnp.max(size, axis=1, keepdims=True), 1e-30)
    exponent = jnp.ceil(jnp.log2(most) * 8.0).astype(jnp.int32)
    root = jnp.sqrt(size / code_scale(exponent))
    level = jnp.minimum(root * CODE_TOP + 0.5, CODE_TOP).astype(jnp.int32)
    codes_ref[:, 0:width] = jnp.where(panels < 0, -level, level).astype(jnp.int16)
    codes_ref[:, width:] = jnp.broadcast_to(exponent, (height, 128)).astype(jnp.int16)

    chosen = jnp.concatenate([chosen_first_ref[...], chosen_second_ref[...]], axis=1)
    column = lax.broadcasted_iota(jnp.int32, (width, chosen.shape[1]), 0)
    onehot = (column == chosen).astype(f32).astype(bf16)
    high = panels.astype(bf16)
    rest = panels - high.astype(f32)
    middle = rest.astype(bf16)
    low = (rest - middle.astype(f32)).astype(bf16)
    pieces = dot(jnp.concatenate([high, middle, low], axis=0), onehot)
    slots_ref[0 : 3 * height, :] = pieces.astype(bf16)
    live = jnp.broadcast_to((chosen >= 0).astype(f32), (height, chosen.shape[1]))
    slots_ref[3 * height :, :] = live.astype(bf16)


def prepare(first, second, chosen_first, chosen_second):
    height, width = 2 * first.shape[0], first.shape[1]
    slots = 2 * chosen_first.shape[1]
    return pl.pallas_call(
        prepare_kernel,
        out_shape=(
            jax.ShapeDtypeStruct((height, width + 128), jnp.int16),
            jax.ShapeDtypeStruct((4 * height, slots), bf16),
        ),
        in_specs=[vmem_spec()] * 4,
        out_specs=(vmem_spec(), vmem_spec()),
        name="prepare",
    )(first, second, chosen_first, chosen_second)


def extract_kernel(weights_ref, chosen_first_ref, chosen_second_ref, out_ref, acc):
    step = pl.program_id(0)
    tile = weights_ref.shape[1]
    chosen = jnp.concatenate([chosen_first_ref[...], chosen_second_ref[...]], axis=1)
    column = lax.broadcasted_iota(jnp.int32, (tile, chosen.shape[1]), 0) + step * tile
    share = dot(weights_ref[...], (column == chosen).astype(f32).astype(bf16))

    @pl.when(step == 0)
    def _():
        acc[...] = share

    @pl.when(step > 0)
    def _():
        acc[...] += share

    @pl.when(step == pl.num_programs(0) - 1)
    def _():
        out_ref[...] = acc[...].astype(bf16)


def extract(weights, chosen_first, chosen_second):
    rows, width = weights.shape
    tile = 1024
    half = chosen_first.shape[1]
    return pl.pallas_call(
        extract_kernel,
        out_shape=jax.ShapeDtypeStruct((rows, 2 * half), bf16),
        grid=(width // tile,),
        in_specs=[
            pl.BlockSpec((rows, tile), lambda i: (0, i)),
            pl.BlockSpec((1, half), lambda i: (0, 0)),
            pl.BlockSpec((1, half), lambda i: (0, 0)),
        ],
        out_specs=pl.BlockSpec((rows, 2 * half), lambda i: (0, 0)),
        scratch_shapes=[VMEM((rows, 2 * half), f32)],
        name="extract",
    )(weights, chosen_first, chosen_second)


def mover(place, order):
    target = lax.broadcasted_iota(jnp.int32, (order, place.shape[1]), 0)
    return (target == place).astype(f32).astype(bf16)


def against(a, b):
    return lax.dot_general(a, b, (((1,), (1,)), ((), ())), preferred_element_type=f32)


def compact_kernel(near_ref, far_ref, entries_ref, places_ref):
    height, order = entries_ref.shape
    slots = near_ref.shape[1]
    half = slots // 2
    total = 4 * height
    per_device = height // 2
    me = lax.axis_index("col")
    lane = lax.broadcasted_iota(jnp.int32, (1, slots), 1)
    in_second = lane >= half
    slot = jnp.where(in_second, lane - half, lane)
    group = near_ref.shape[0] // total

    def block(index, start, stop):
        ref = near_ref if index < group else far_ref
        at = (index % group) * total
        return ref[at + start : at + stop, :]

    live = [block(i, 3 * height, total).astype(f32)[0:1, :] for i in range(len(OWNER_ORDER))]
    firsts = [jnp.sum(jnp.where(in_second, 0.0, x), axis=1, keepdims=True) for x in live]
    seconds = [jnp.sum(jnp.where(in_second, x, 0.0), axis=1, keepdims=True) for x in live]
    result = None
    for i, relative in enumerate(OWNER_ORDER):
        base_first = jnp.zeros((1, 1), f32)
        base_second = jnp.zeros((1, 1), f32)
        for j, other in enumerate(OWNER_ORDER):
            before = ((me ^ other) < (me ^ relative)).astype(f32)
            base_first = base_first + before * firsts[j]
            base_second = base_second + before * seconds[j]
        position = jnp.where(in_second, base_second, base_first).astype(jnp.int32) + slot
        place = (
            (position // per_device) * height
            + jnp.where(in_second, per_device, 0)
            + position % per_device
        )
        place = jnp.where(live[i] > 0.5, place, -1)
        places_ref[i : i + 1, :] = place
        share = against(block(i, 0, 3 * height), mover(place, order))
        result = share if result is None else result + share
    high = result[0:height, :]
    middle = result[height : 2 * height, :]
    entries_ref[...] = high + (middle + result[2 * height : 3 * height, :])


def compact(near, far, height, order):
    return pl.pallas_call(
        compact_kernel,
        out_shape=(
            jax.ShapeDtypeStruct((height, order), f32),
            jax.ShapeDtypeStruct((len(OWNER_ORDER), near.shape[1]), jnp.int32),
        ),
        in_specs=[vmem_spec()] * 2,
        out_specs=(vmem_spec(), vmem_spec()),
        name="compact",
    )(near, far)


def place_kernel(near_ref, far_ref, places_ref, columns_ref):
    rows, order = columns_ref.shape
    group = near_ref.shape[0] // rows
    result = None
    for i in range(len(OWNER_ORDER)):
        ref = near_ref if i < group else far_ref
        at = (i % group) * rows
        share = against(ref[at : at + rows, :], mover(places_ref[i : i + 1, :], order))
        result = share if result is None else result + share
    columns_ref[...] = result.astype(bf16)


def place(near, far, places, rows, order):
    return pl.pallas_call(
        place_kernel,
        out_shape=jax.ShapeDtypeStruct((rows, order), bf16),
        in_specs=[vmem_spec()] * 3,
        out_specs=vmem_spec(),
        name="place",
    )(near, far, places)


def solve_kernel(own_ref, sibling_ref, columns_ref, high_ref, low_ref, entries_ref, stacked, inverse):
    order = entries_ref.shape[0]
    rows = columns_ref.shape[0]
    me = lax.axis_index("row")
    height = order // len(ENTRY_ORDER)
    for i, relative in enumerate(ENTRY_ORDER):
        ref = own_ref if i < len(ENTRY_ORDER) // 2 else sibling_ref
        at = (i % (len(ENTRY_ORDER) // 2)) * height
        start = pl.multiple_of((me ^ relative) * height, height)
        entries_ref[pl.ds(start, height), :] = ref[at : at + height, :]
    row = lax.broadcasted_iota(jnp.int32, (order, order), 0)
    col = lax.broadcasted_iota(jnp.int32, (order, order), 1)
    entries = entries_ref[...]
    diagonal = jnp.where(row == col, entries, 0.0)
    scale_row = lax.rsqrt(jnp.sum(diagonal, axis=0, keepdims=True))
    scale_col = lax.rsqrt(jnp.sum(diagonal, axis=1, keepdims=True))
    unit = entries * scale_col * scale_row
    rest = jnp.where(row == col, 1.0 - unit, -unit)
    stacked[0:rows, :] = columns_ref[...].astype(f32) * scale_row
    stacked[rows:, :] = rest

    def bound():
        power = stacked[rows:, :]
        return jnp.sum(power * power)

    def going(state):
        count, left = state
        return jnp.logical_and(count < DOUBLINGS, jnp.logical_not(left < TOLERANCE))

    def double(state):
        count, _ = state
        power = stacked[rows:, :]
        result = product(stacked[...], power)
        stacked[0:rows, :] += result[0:rows, :]
        stacked[rows:, :] = result[rows:, :]
        return count + 1, bound()

    _, left = lax.while_loop(going, double, (jnp.int32(0), bound()))
    settled = left < TOLERANCE

    def finish(solved):
        index = lax.broadcasted_iota(jnp.int32, (1, order), 1)
        source = jnp.zeros((1, order), jnp.int32)
        for i, relative in enumerate(PANEL_ORDER):
            source = jnp.where(index // height == i, (me ^ relative) * height, source)
        arrange = (row == source + index % height).astype(f32).astype(bf16)
        high, low = halves(solved * (scale_row * (1.0 / (CODE_TOP * CODE_TOP))))
        high_ref[...] = dot(high, arrange).astype(bf16)
        low_ref[...] = dot(low, arrange).astype(bf16)

    @pl.when(settled)
    def _():
        solved = stacked[0:rows, :]
        finish(solved + product(solved, stacked[rows:, :]))

    @pl.when(jnp.logical_not(settled))
    def _():
        inverse[...] = entries_ref[...] * scale_col * scale_row

        def pivot(k, carry):
            lanes = lax.broadcasted_iota(jnp.int32, (1, order), 1)
            pivot_row = inverse[pl.ds(k, 1), :]
            head = jnp.sum(jnp.where(lanes == k, pivot_row, 0.0), axis=1, keepdims=True)
            pivot_row = jnp.where(lanes == k, 1.0, pivot_row) / head
            everything = inverse[...]
            column = jnp.sum(jnp.where(col == k, everything, 0.0), axis=1, keepdims=True)
            kept = jnp.where(col == k, 0.0, everything)
            inverse[...] = kept - column * pivot_row
            inverse[pl.ds(k, 1), :] = pivot_row
            return carry

        lax.fori_loop(0, order, pivot, 0)
        whole = entries_ref[...] * scale_col * scale_row
        wanted = columns_ref[...].astype(f32) * scale_row

        def exact(a, b):
            return jnp.dot(a, b, precision=lax.Precision.HIGHEST, preferred_element_type=f32)

        solved = exact(wanted, inverse[...])
        solved = solved + exact(wanted - exact(solved, whole), inverse[...])
        finish(solved)


def solve(own, sibling, columns):
    rows, order = columns.shape
    return pl.pallas_call(
        solve_kernel,
        out_shape=(jax.ShapeDtypeStruct((rows, order), bf16),) * 2,
        in_specs=[vmem_spec()] * 3,
        out_specs=(vmem_spec(), vmem_spec()),
        scratch_shapes=[
            VMEM((order, order), f32),
            VMEM((rows + order, order), f32),
            VMEM((order, order), f32),
        ],
        name="solve",
    )(own, sibling, columns)


def update_kernel(weights_ref, high_ref, low_ref, *rest):
    panels, out_ref = rest[:-1], rest[-1]
    tile = weights_ref.shape[1]
    width = panels[0].shape[1] - 128
    start = pl.multiple_of(pl.program_id(0) * tile, tile)
    pieces = []
    for ref in panels:
        scale = code_scale(ref[:, width:].astype(jnp.int32))[:, 0:1]
        code = ref[:, pl.ds(start, tile)].astype(jnp.int32).astype(f32)
        pieces.append(halves(code * jnp.abs(code) * scale))
    panel_high = jnp.concatenate([p[0] for p in pieces], axis=0)
    panel_low = jnp.concatenate([p[1] for p in pieces], axis=0)
    high = high_ref[...]
    change = dot(high, panel_high) + (dot(high, panel_low) + dot(low_ref[...], panel_high))
    out_ref[...] = (weights_ref[...].astype(f32) - change).astype(bf16)


def update(weights, high, low, panels):
    rows, width = weights.shape
    order = high.shape[1]
    tile = 512
    return pl.pallas_call(
        update_kernel,
        out_shape=jax.ShapeDtypeStruct((rows, width), bf16),
        grid=(width // tile,),
        in_specs=[
            pl.BlockSpec((rows, tile), lambda i: (0, i)),
            pl.BlockSpec((rows, order), lambda i: (0, 0)),
            pl.BlockSpec((rows, order), lambda i: (0, 0)),
        ]
        + [vmem_spec()] * len(panels),
        out_specs=pl.BlockSpec((rows, tile), lambda i: (0, i)),
        name="update",
    )(weights, high, low, *panels)


def swap(value, axis, relative):
    size = lax.axis_size(axis)
    return lax.ppermute(value, axis, [(i, i ^ relative) for i in range(size)])


def grow(value, axis, relative):
    return jnp.concatenate([value, swap(value, axis, relative)], axis=0)


def on_device(weights, panel_first, panel_second, removed_first, removed_second):
    rows = weights.shape[0]
    height = 2 * panel_first.shape[0]
    order = height * lax.axis_size("row")
    chosen_first = removed_first[None, :]
    chosen_second = removed_second[None, :]
    codes, slots = prepare(panel_first, panel_second, chosen_first, chosen_second)

    near = grow(grow(slots, "col", Z_HALF), "col", X_ONE)
    far = swap(near, "col", X_THREE)
    entries, places = compact(near, far, height, order)
    entries = grow(grow(grow(grow(entries, "row", Z_ONE), "row", Z_TWO), "row", Y_ONE), "row", Y_THREE)
    sibling = swap(entries, "row", CORE)

    mine = extract(weights, chosen_first, chosen_second)
    mine_near = grow(grow(mine, "col", Z_HALF), "col", X_ONE)
    mine_far = swap(mine_near, "col", X_THREE)
    columns = place(mine_near, mine_far, places, rows, order)

    even = grow(grow(codes, "row", Z_ONE), "row", Y_ONE)
    even_far = swap(even, "row", Y_THREE)
    odd = jnp.concatenate([swap(codes, "row", Z_TWO), swap(codes, "row", Z_THREE)], axis=0)
    odd = grow(odd, "row", Y_THREE)
    odd_far = swap(odd, "row", Y_ONE)
    panels = [even, even_far, odd, odd_far]
    panels = panels + [swap(p, "row", CORE) for p in panels]

    high, low = solve(entries, sibling, columns)
    return update(weights, high, low, panels)


def solution(mesh):
    return jax.shard_map(
        on_device,
        mesh=mesh,
        in_specs=(P("row", "col"), P("row", "col"), P("row", "col"), P("col"), P("col")),
        out_specs=P("row", "col"),
        check_vma=False,
    )
```

```python
import jax
import jax.numpy as jnp
from jax import lax
from jax.experimental import pallas as pl
from jax.experimental.pallas import tpu as pltpu
from jax.sharding import PartitionSpec as P


f32 = jnp.float32
bf16 = jnp.bfloat16
VMEM = pltpu.VMEM
MIB = 1 << 20
TOLERANCE = 3e-5
DOUBLINGS = 6
CODE_TOP = 32767.0
PARTS = 4
CORE, Y_ONE, Y_THREE, Z_ONE, Z_TWO, Z_THREE = 1, 2, 6, 8, 16, 24
X_ONE, X_THREE, Z_HALF = 1, 3, 4
OWNER_ORDER = (0, 4, 1, 5, 3, 7, 2, 6)
ENTRY_ORDER = tuple(c + y * 2 + z * 8 for c in (0, 1) for y in (0, 1, 3, 2) for z in range(4))
PANEL_ORDER = tuple(
    c + y * 2 + z * 8
    for c in (0, 1)
    for ys, zs in (((0, 1, 3, 2), (0, 1)), ((0, 3, 1, 2), (2, 3)))
    for y in ys
    for z in zs
)


def vmem_spec():
    return pl.BlockSpec(memory_space=VMEM)


def halves(value):
    high = value.astype(bf16)
    low = (value - high.astype(f32)).astype(bf16)
    return high, low


def dot(a, b):
    return jnp.dot(a, b, preferred_element_type=f32)


def product(a, b):
    a_high, a_low = halves(a)
    b_high, b_low = halves(b)
    return dot(a_high, b_high) + (dot(a_high, b_low) + dot(a_low, b_high))


def code_scale(exponent):
    return jnp.exp2(exponent.astype(f32) * 0.125)


def prepare_kernel(
    first_hbm,
    second_hbm,
    chosen_first_hbm,
    chosen_second_hbm,
    weights_hbm,
    codes_ref,
    slots_ref,
    mine_ref,
    panels_ref,
    chosen_first_ref,
    chosen_second_ref,
    weights_ref,
    onehot_ref,
    arrived,
):
    half, width = first_hbm.shape
    height = 2 * half
    part = width // PARTS
    moves = [
        (chosen_first_hbm, chosen_first_ref),
        (chosen_second_hbm, chosen_second_ref),
        (first_hbm, panels_ref.at[0:half]),
        (second_hbm, panels_ref.at[half:height]),
    ]
    for i in range(PARTS):
        columns = pl.ds(i * part, part)
        moves.append((weights_hbm.at[:, columns], weights_ref.at[:, columns]))
    copies = [
        pltpu.make_async_copy(source, target, arrived.at[i])
        for i, (source, target) in enumerate(moves)
    ]
    for copy in copies:
        copy.start()
    for copy in copies[0:4]:
        copy.wait()
    panels = panels_ref[...]
    size = jnp.abs(panels)
    most = jnp.maximum(jnp.max(size, axis=1, keepdims=True), 1e-30)
    exponent = jnp.ceil(jnp.log2(most) * 8.0).astype(jnp.int32)
    root = jnp.sqrt(size / code_scale(exponent))
    level = jnp.minimum(root * CODE_TOP + 0.5, CODE_TOP).astype(jnp.int32)
    codes_ref[:, 0:width] = jnp.where(panels < 0, -level, level).astype(jnp.int16)
    codes_ref[:, width:] = jnp.broadcast_to(exponent, (height, 128)).astype(jnp.int16)

    chosen = jnp.concatenate([chosen_first_ref[...], chosen_second_ref[...]], axis=1)
    column = lax.broadcasted_iota(jnp.int32, (width, chosen.shape[1]), 0)
    onehot_ref[...] = (column == chosen).astype(f32).astype(bf16)
    high = panels.astype(bf16)
    rest = panels - high.astype(f32)
    middle = rest.astype(bf16)
    low = (rest - middle.astype(f32)).astype(bf16)
    pieces = dot(jnp.concatenate([high, middle, low], axis=0), onehot_ref[...])
    slots_ref[0 : 3 * height, :] = pieces.astype(bf16)
    live = jnp.broadcast_to((chosen >= 0).astype(f32), (height, chosen.shape[1]))
    slots_ref[3 * height :, :] = live.astype(bf16)

    taken = None
    for i, copy in enumerate(copies[4:]):
        copy.wait()
        at = i * part
        share = dot(weights_ref[:, at : at + part], onehot_ref[at : at + part, :])
        taken = share if taken is None else taken + share
    mine_ref[...] = taken.astype(bf16)


def prepare(first, second, chosen_first, chosen_second, weights):
    height, width = 2 * first.shape[0], first.shape[1]
    rows = weights.shape[0]
    slots = 2 * chosen_first.shape[1]
    return pl.pallas_call(
        prepare_kernel,
        out_shape=(
            jax.ShapeDtypeStruct((height, width + 128), jnp.int16),
            jax.ShapeDtypeStruct((4 * height, slots), bf16),
            jax.ShapeDtypeStruct((rows, slots), bf16),
        ),
        in_specs=[pl.BlockSpec(memory_space=pltpu.HBM)] * 5,
        out_specs=(vmem_spec(),) * 3,
        scratch_shapes=[
            VMEM((height, width), f32),
            VMEM(chosen_first.shape, jnp.int32),
            VMEM(chosen_second.shape, jnp.int32),
            VMEM((rows, width), bf16),
            VMEM((width, slots), bf16),
            pltpu.SemaphoreType.DMA((4 + PARTS,)),
        ],
        name="prepare",
        compiler_params=pltpu.CompilerParams(vmem_limit_bytes=56360960),
    )(first, second, chosen_first, chosen_second, weights)


def mover(place, order):
    target = lax.broadcasted_iota(jnp.int32, (order, place.shape[1]), 0)
    return (target == place).astype(f32).astype(bf16)


def against(a, b):
    return lax.dot_general(a, b, (((1,), (1,)), ((), ())), preferred_element_type=f32)


def compact_kernel(near_ref, far_ref, entries_ref, places_ref):
    height, order = entries_ref.shape
    slots = near_ref.shape[1]
    half = slots // 2
    total = 4 * height
    per_device = height // 2
    me = lax.axis_index("col")
    lane = lax.broadcasted_iota(jnp.int32, (1, slots), 1)
    in_second = lane >= half
    slot = jnp.where(in_second, lane - half, lane)
    group = near_ref.shape[0] // total

    def block(index, start, stop):
        ref = near_ref if index < group else far_ref
        at = (index % group) * total
        return ref[at + start : at + stop, :]

    live = [block(i, 3 * height, total).astype(f32)[0:1, :] for i in range(len(OWNER_ORDER))]
    firsts = [jnp.sum(jnp.where(in_second, 0.0, x), axis=1, keepdims=True) for x in live]
    seconds = [jnp.sum(jnp.where(in_second, x, 0.0), axis=1, keepdims=True) for x in live]
    result = None
    for i, relative in enumerate(OWNER_ORDER):
        base_first = jnp.zeros((1, 1), f32)
        base_second = jnp.zeros((1, 1), f32)
        for j, other in enumerate(OWNER_ORDER):
            before = ((me ^ other) < (me ^ relative)).astype(f32)
            base_first = base_first + before * firsts[j]
            base_second = base_second + before * seconds[j]
        position = jnp.where(in_second, base_second, base_first).astype(jnp.int32) + slot
        place = (
            (position // per_device) * height
            + jnp.where(in_second, per_device, 0)
            + position % per_device
        )
        place = jnp.where(live[i] > 0.5, place, -1)
        places_ref[i : i + 1, :] = place
        share = against(block(i, 0, 3 * height), mover(place, order))
        result = share if result is None else result + share
    high = result[0:height, :]
    middle = result[height : 2 * height, :]
    entries_ref[...] = high + (middle + result[2 * height : 3 * height, :])


def compact(near, far, height, order):
    return pl.pallas_call(
        compact_kernel,
        out_shape=(
            jax.ShapeDtypeStruct((height, order), f32),
            jax.ShapeDtypeStruct((len(OWNER_ORDER), near.shape[1]), jnp.int32),
        ),
        in_specs=[vmem_spec()] * 2,
        out_specs=(vmem_spec(), vmem_spec()),
        name="compact",
        compiler_params=pltpu.CompilerParams(vmem_limit_bytes=8 * MIB),
    )(near, far)


def place_kernel(near_ref, far_ref, places_ref, columns_ref):
    rows, order = columns_ref.shape
    group = near_ref.shape[0] // rows
    result = None
    for i in range(len(OWNER_ORDER)):
        ref = near_ref if i < group else far_ref
        at = (i % group) * rows
        share = against(ref[at : at + rows, :], mover(places_ref[i : i + 1, :], order))
        result = share if result is None else result + share
    columns_ref[...] = result.astype(bf16)


def place(near, far, places, rows, order):
    return pl.pallas_call(
        place_kernel,
        out_shape=jax.ShapeDtypeStruct((rows, order), bf16),
        in_specs=[vmem_spec()] * 3,
        out_specs=vmem_spec(),
        name="place",
        compiler_params=pltpu.CompilerParams(vmem_limit_bytes=8 * MIB),
    )(near, far, places)


def solve_kernel(own_ref, sibling_ref, columns_ref, high_ref, low_ref, entries_ref, stacked, inverse):
    order = entries_ref.shape[0]
    rows = columns_ref.shape[0]
    me = lax.axis_index("row")
    height = order // len(ENTRY_ORDER)
    for i, relative in enumerate(ENTRY_ORDER):
        ref = own_ref if i < len(ENTRY_ORDER) // 2 else sibling_ref
        at = (i % (len(ENTRY_ORDER) // 2)) * height
        start = pl.multiple_of((me ^ relative) * height, height)
        entries_ref[pl.ds(start, height), :] = ref[at : at + height, :]
    row = lax.broadcasted_iota(jnp.int32, (order, order), 0)
    col = lax.broadcasted_iota(jnp.int32, (order, order), 1)
    entries = entries_ref[...]
    diagonal = jnp.where(row == col, entries, 0.0)
    scale_row = lax.rsqrt(jnp.sum(diagonal, axis=0, keepdims=True))
    scale_col = lax.rsqrt(jnp.sum(diagonal, axis=1, keepdims=True))
    unit = entries * scale_col * scale_row
    rest = jnp.where(row == col, 1.0 - unit, -unit)
    stacked[0:rows, :] = columns_ref[...].astype(f32) * scale_row
    stacked[rows:, :] = rest

    def bound():
        power = stacked[rows:, :]
        return jnp.sum(power * power)

    def going(state):
        count, left = state
        return jnp.logical_and(count < DOUBLINGS, jnp.logical_not(left < TOLERANCE))

    def double(state):
        count, _ = state
        power = stacked[rows:, :]
        result = product(stacked[...], power)
        stacked[0:rows, :] += result[0:rows, :]
        stacked[rows:, :] = result[rows:, :]
        return count + 1, bound()

    _, left = lax.while_loop(going, double, (jnp.int32(0), bound()))
    settled = left < TOLERANCE

    def finish(solved):
        index = lax.broadcasted_iota(jnp.int32, (1, order), 1)
        source = jnp.zeros((1, order), jnp.int32)
        for i, relative in enumerate(PANEL_ORDER):
            source = jnp.where(index // height == i, (me ^ relative) * height, source)
        arrange = (row == source + index % height).astype(f32).astype(bf16)
        high, low = halves(solved * (scale_row * (1.0 / (CODE_TOP * CODE_TOP))))
        high_ref[...] = dot(high, arrange).astype(bf16)
        low_ref[...] = dot(low, arrange).astype(bf16)

    @pl.when(settled)
    def _():
        solved = stacked[0:rows, :]
        finish(solved + product(solved, stacked[rows:, :]))

    @pl.when(jnp.logical_not(settled))
    def _():
        inverse[...] = entries_ref[...] * scale_col * scale_row

        def pivot(k, carry):
            lanes = lax.broadcasted_iota(jnp.int32, (1, order), 1)
            pivot_row = inverse[pl.ds(k, 1), :]
            head = jnp.sum(jnp.where(lanes == k, pivot_row, 0.0), axis=1, keepdims=True)
            pivot_row = jnp.where(lanes == k, 1.0, pivot_row) / head
            everything = inverse[...]
            column = jnp.sum(jnp.where(col == k, everything, 0.0), axis=1, keepdims=True)
            kept = jnp.where(col == k, 0.0, everything)
            inverse[...] = kept - column * pivot_row
            inverse[pl.ds(k, 1), :] = pivot_row
            return carry

        lax.fori_loop(0, order, pivot, 0)
        whole = entries_ref[...] * scale_col * scale_row
        wanted = columns_ref[...].astype(f32) * scale_row

        def exact(a, b):
            return jnp.dot(a, b, precision=lax.Precision.HIGHEST, preferred_element_type=f32)

        solved = exact(wanted, inverse[...])
        solved = solved + exact(wanted - exact(solved, whole), inverse[...])
        finish(solved)


def solve(own, sibling, columns):
    rows, order = columns.shape
    return pl.pallas_call(
        solve_kernel,
        out_shape=(jax.ShapeDtypeStruct((rows, order), bf16),) * 2,
        in_specs=[vmem_spec()] * 3,
        out_specs=(vmem_spec(), vmem_spec()),
        scratch_shapes=[
            VMEM((order, order), f32),
            VMEM((rows + order, order), f32),
            VMEM((order, order), f32),
        ],
        name="solve",
        compiler_params=pltpu.CompilerParams(vmem_limit_bytes=24 * MIB),
    )(own, sibling, columns)


def update_kernel(weights_ref, high_ref, low_ref, *rest):
    panels, out_ref = rest[:-1], rest[-1]
    tile = weights_ref.shape[1]
    width = panels[0].shape[1] - 128
    start = pl.multiple_of(pl.program_id(0) * tile, tile)
    pieces = []
    for ref in panels:
        scale = code_scale(ref[:, width:].astype(jnp.int32))[:, 0:1]
        code = ref[:, pl.ds(start, tile)].astype(jnp.int32).astype(f32)
        pieces.append(halves(code * jnp.abs(code) * scale))
    panel_high = jnp.concatenate([p[0] for p in pieces], axis=0)
    panel_low = jnp.concatenate([p[1] for p in pieces], axis=0)
    high = high_ref[...]
    change = dot(high, panel_high) + (dot(high, panel_low) + dot(low_ref[...], panel_high))
    out_ref[...] = (weights_ref[...].astype(f32) - change).astype(bf16)


def update(weights, high, low, panels):
    rows, width = weights.shape
    order = high.shape[1]
    tile = 512
    return pl.pallas_call(
        update_kernel,
        out_shape=jax.ShapeDtypeStruct((rows, width), bf16),
        grid=(width // tile,),
        in_specs=[
            pl.BlockSpec((rows, tile), lambda i: (0, i)),
            pl.BlockSpec((rows, order), lambda i: (0, 0)),
            pl.BlockSpec((rows, order), lambda i: (0, 0)),
        ]
        + [vmem_spec()] * len(panels),
        out_specs=pl.BlockSpec((rows, tile), lambda i: (0, i)),
        name="update",
        compiler_params=pltpu.CompilerParams(vmem_limit_bytes=24 * MIB),
    )(weights, high, low, *panels)


def swap(value, axis, relative):
    size = lax.axis_size(axis)
    return lax.ppermute(value, axis, [(i, i ^ relative) for i in range(size)])


def grow(value, axis, relative):
    return join(value, swap(value, axis, relative))


def join(*values):
    return lax.optimization_barrier(jnp.concatenate(values, axis=0))


def prune(weights, panel_first, panel_second, removed_first, removed_second):
    rows = weights.shape[0]
    height = 2 * panel_first.shape[0]
    order = height * lax.axis_size("row")
    chosen_first = removed_first[None, :]
    chosen_second = removed_second[None, :]
    codes, slots, mine = prepare(panel_first, panel_second, chosen_first, chosen_second, weights)

    near = grow(grow(slots, "col", Z_HALF), "col", X_ONE)
    far = swap(near, "col", X_THREE)
    entries, places = compact(near, far, height, order)
    entries = grow(entries, "row", Z_ONE)
    entries = grow(entries, "row", Z_TWO)
    entries = grow(entries, "row", Y_ONE)
    entries = grow(entries, "row", Y_THREE)
    sibling = swap(entries, "row", CORE)

    mine_near = grow(grow(mine, "col", Z_HALF), "col", X_ONE)
    mine_far = swap(mine_near, "col", X_THREE)
    columns = place(mine_near, mine_far, places, rows, order)

    even = grow(codes, "row", Z_ONE)
    even_one = swap(even, "row", Y_ONE)
    even_three = swap(even, "row", Y_THREE)
    even_two = swap(even_one, "row", Y_THREE)
    odd = join(swap(codes, "row", Z_TWO), swap(codes, "row", Z_THREE))
    odd_three = swap(odd, "row", Y_THREE)
    odd_one = swap(odd, "row", Y_ONE)
    odd_two = swap(odd_three, "row", Y_ONE)
    panels = [even, even_one, even_three, even_two, odd, odd_three, odd_one, odd_two]
    panels = panels + [swap(p, "row", CORE) for p in panels]

    high, low = solve(entries, sibling, columns)
    return update(weights, high, low, panels)


def solution(mesh):
    return jax.shard_map(
        prune,
        mesh=mesh,
        in_specs=(P("row", "col"), P("row", "col"), P("row", "col"), P("col"), P("col")),
        out_specs=P("row", "col"),
        check_vma=False,
    )
```

```python
import jax
import jax.numpy as jnp
from jax import lax
from jax.experimental import pallas as pl
from jax.experimental.pallas import tpu as pltpu
from jax.sharding import PartitionSpec as P


f32 = jnp.float32
bf16 = jnp.bfloat16
VMEM = pltpu.VMEM
MIB = 1 << 20
TOLERANCE = 3e-5
DOUBLINGS = 6
RESIDUAL = 1e-5
CODE_TOP = 32767.0
PARTS = 4
TILE = 512
CORE, Y_ONE, Y_THREE, Z_ONE, Z_TWO, Z_THREE = 1, 2, 6, 8, 16, 24
X_ONE, X_THREE, Z_HALF = 1, 3, 4
OWNER_ORDER = (0, 4, 1, 5, 3, 7, 2, 6)
ENTRY_ORDER = tuple(c + y * 2 + z * 8 for c in (0, 1) for y in (0, 1, 3, 2) for z in range(4))
PANEL_ORDER = tuple(
    c + y * 2 + z * 8
    for c in (0, 1)
    for ys, zs in (((0, 1, 3, 2), (0, 1)), ((0, 3, 1, 2), (2, 3)))
    for y in ys
    for z in zs
)


def vmem_spec():
    return pl.BlockSpec(memory_space=VMEM)


def halves(value):
    high = value.astype(bf16)
    low = (value - high.astype(f32)).astype(bf16)
    return high, low


def dot(a, b):
    return jnp.dot(a, b, preferred_element_type=f32)


def code_scale(exponent):
    return jnp.exp2(exponent.astype(f32) * 0.125)


def prepare_kernel(
    first_hbm,
    second_hbm,
    chosen_first_hbm,
    chosen_second_hbm,
    weights_hbm,
    codes_ref,
    slots_ref,
    mine_ref,
    panels_ref,
    chosen_first_ref,
    chosen_second_ref,
    weights_ref,
    onehot_ref,
    arrived,
):
    half, width = first_hbm.shape
    height = 2 * half
    part = width // PARTS
    moves = [
        (chosen_first_hbm, chosen_first_ref),
        (chosen_second_hbm, chosen_second_ref),
        (first_hbm, panels_ref.at[0:half]),
        (second_hbm, panels_ref.at[half:height]),
    ]
    for i in range(PARTS):
        columns = pl.ds(i * part, part)
        moves.append((weights_hbm.at[:, columns], weights_ref.at[:, columns]))
    copies = [
        pltpu.make_async_copy(source, target, arrived.at[i])
        for i, (source, target) in enumerate(moves)
    ]
    for copy in copies:
        copy.start()
    for copy in copies[0:4]:
        copy.wait()
    panels = panels_ref[...]
    size = jnp.abs(panels)
    most = jnp.maximum(jnp.max(size, axis=1, keepdims=True), 1e-30)
    exponent = jnp.ceil(jnp.log2(most) * 8.0).astype(jnp.int32)
    root = jnp.sqrt(size / code_scale(exponent))
    level = jnp.minimum(root * CODE_TOP + 0.5, CODE_TOP).astype(jnp.int32)
    codes_ref[:, 0:width] = jnp.where(panels < 0, -level, level).astype(jnp.int16)
    codes_ref[:, width:] = jnp.broadcast_to(exponent, (height, 128)).astype(jnp.int16)

    chosen = jnp.concatenate([chosen_first_ref[...], chosen_second_ref[...]], axis=1)
    column = lax.broadcasted_iota(jnp.int32, (width, chosen.shape[1]), 0)
    onehot_ref[...] = (column == chosen).astype(f32).astype(bf16)
    high = panels.astype(bf16)
    rest = panels - high.astype(f32)
    middle = rest.astype(bf16)
    low = (rest - middle.astype(f32)).astype(bf16)
    pieces = dot(jnp.concatenate([high, middle, low], axis=0), onehot_ref[...])
    slots_ref[0 : 3 * height, :] = pieces.astype(bf16)
    live = jnp.broadcast_to((chosen >= 0).astype(f32), (height, chosen.shape[1]))
    slots_ref[3 * height :, :] = live.astype(bf16)

    taken = None
    for i, copy in enumerate(copies[4:]):
        copy.wait()
        at = i * part
        share = dot(weights_ref[:, at : at + part], onehot_ref[at : at + part, :])
        taken = share if taken is None else taken + share
    mine_ref[...] = taken.astype(bf16)


def prepare(first, second, chosen_first, chosen_second, weights):
    height, width = 2 * first.shape[0], first.shape[1]
    rows = weights.shape[0]
    slots = 2 * chosen_first.shape[1]
    return pl.pallas_call(
        prepare_kernel,
        out_shape=(
            jax.ShapeDtypeStruct((height, width + 128), jnp.int16),
            jax.ShapeDtypeStruct((4 * height, slots), bf16),
            jax.ShapeDtypeStruct((rows, slots), bf16),
        ),
        in_specs=[pl.BlockSpec(memory_space=pltpu.HBM)] * 5,
        out_specs=(vmem_spec(),) * 3,
        scratch_shapes=[
            VMEM((height, width), f32),
            VMEM(chosen_first.shape, jnp.int32),
            VMEM(chosen_second.shape, jnp.int32),
            VMEM((rows, width), bf16),
            VMEM((width, slots), bf16),
            pltpu.SemaphoreType.DMA((4 + PARTS,)),
        ],
        name="prepare",
        compiler_params=pltpu.CompilerParams(vmem_limit_bytes=56360960),
    )(first, second, chosen_first, chosen_second, weights)


def mover(place, order):
    target = lax.broadcasted_iota(jnp.int32, (order, place.shape[1]), 0)
    return (target == place).astype(f32).astype(bf16)


def against(a, b):
    return lax.dot_general(a, b, (((1,), (1,)), ((), ())), preferred_element_type=f32)


def compact_kernel(near_ref, far_ref, entries_ref, places_ref):
    height, order = entries_ref.shape
    slots = near_ref.shape[1]
    half = slots // 2
    total = 4 * height
    per_device = height // 2
    me = lax.axis_index("col")
    lane = lax.broadcasted_iota(jnp.int32, (1, slots), 1)
    in_second = lane >= half
    slot = jnp.where(in_second, lane - half, lane)
    group = near_ref.shape[0] // total

    def block(index, start, stop):
        ref = near_ref if index < group else far_ref
        at = (index % group) * total
        return ref[at + start : at + stop, :]

    live = [block(i, 3 * height, total).astype(f32)[0:1, :] for i in range(len(OWNER_ORDER))]
    firsts = [jnp.sum(jnp.where(in_second, 0.0, x), axis=1, keepdims=True) for x in live]
    seconds = [jnp.sum(jnp.where(in_second, x, 0.0), axis=1, keepdims=True) for x in live]
    result = None
    for i, relative in enumerate(OWNER_ORDER):
        base_first = jnp.zeros((1, 1), f32)
        base_second = jnp.zeros((1, 1), f32)
        for j, other in enumerate(OWNER_ORDER):
            before = ((me ^ other) < (me ^ relative)).astype(f32)
            base_first = base_first + before * firsts[j]
            base_second = base_second + before * seconds[j]
        position = jnp.where(in_second, base_second, base_first).astype(jnp.int32) + slot
        place = (
            (position // per_device) * height
            + jnp.where(in_second, per_device, 0)
            + position % per_device
        )
        place = jnp.where(live[i] > 0.5, place, -1)
        places_ref[i : i + 1, :] = place
        share = against(block(i, 0, 3 * height), mover(place, order))
        result = share if result is None else result + share
    high = result[0:height, :]
    middle = result[height : 2 * height, :]
    entries_ref[...] = high + (middle + result[2 * height : 3 * height, :])


def compact(near, far, height, order):
    return pl.pallas_call(
        compact_kernel,
        out_shape=(
            jax.ShapeDtypeStruct((height, order), f32),
            jax.ShapeDtypeStruct((len(OWNER_ORDER), near.shape[1]), jnp.int32),
        ),
        in_specs=[vmem_spec()] * 2,
        out_specs=(vmem_spec(), vmem_spec()),
        name="compact",
        compiler_params=pltpu.CompilerParams(vmem_limit_bytes=8 * MIB),
    )(near, far)


def place_kernel(near_ref, far_ref, places_ref, columns_ref):
    rows, order = columns_ref.shape
    group = near_ref.shape[0] // rows
    result = None
    for i in range(len(OWNER_ORDER)):
        ref = near_ref if i < group else far_ref
        at = (i % group) * rows
        share = against(ref[at : at + rows, :], mover(places_ref[i : i + 1, :], order))
        result = share if result is None else result + share
    columns_ref[...] = result.astype(bf16)


def place(near, far, places, rows, order):
    return pl.pallas_call(
        place_kernel,
        out_shape=jax.ShapeDtypeStruct((rows, order), bf16),
        in_specs=[vmem_spec()] * 3,
        out_specs=vmem_spec(),
        name="place",
        compiler_params=pltpu.CompilerParams(vmem_limit_bytes=8 * MIB),
    )(near, far, places)


def solve_kernel(
    own_ref, sibling_ref, columns_ref, high_ref, low_ref, entries_ref, value, wanted, powers, rest_low, inverse
):
    order = entries_ref.shape[0]
    rows = columns_ref.shape[0]
    me = lax.axis_index("row")
    height = order // len(ENTRY_ORDER)
    for i, relative in enumerate(ENTRY_ORDER):
        ref = own_ref if i < len(ENTRY_ORDER) // 2 else sibling_ref
        at = (i % (len(ENTRY_ORDER) // 2)) * height
        start = pl.multiple_of((me ^ relative) * height, height)
        entries_ref[pl.ds(start, height), :] = ref[at : at + height, :]
    row = lax.broadcasted_iota(jnp.int32, (order, order), 0)
    col = lax.broadcasted_iota(jnp.int32, (order, order), 1)
    entries = entries_ref[...]
    diagonal = jnp.where(row == col, entries, 0.0)
    scale_row = lax.rsqrt(jnp.sum(diagonal, axis=0, keepdims=True))
    scale_col = lax.rsqrt(jnp.sum(diagonal, axis=1, keepdims=True))
    unit = entries * scale_col * scale_row
    rest = jnp.where(row == col, 1.0 - unit, -unit)
    rest_high = rest.astype(bf16)
    powers[0:order, :] = rest_high
    rest_low[...] = (rest - rest_high.astype(f32)).astype(bf16)
    scaled = columns_ref[...].astype(f32) * scale_row
    wanted[...] = scaled
    value[...] = scaled

    def power(index):
        return powers[pl.ds(pl.multiple_of(index * order, order), order), :]

    def apply(index):
        value[...] += dot(value[...].astype(bf16), power(index))

    def going(state):
        count, left = state
        return jnp.logical_and(count < DOUBLINGS, jnp.logical_not(left < TOLERANCE))

    def double(state):
        count, _ = state
        this = power(count)
        apply(count)
        squared = dot(this, this)
        powers[pl.ds(pl.multiple_of((count + 1) * order, order), order), :] = squared.astype(bf16)
        return count + 1, jnp.sum(squared * squared)

    count, _ = lax.while_loop(going, double, (jnp.int32(0), jnp.sum(rest * rest)))
    apply(count)
    first = value[...]
    first_high, first_low = halves(first)
    through = dot(first_high, power(0)) + (dot(first_high, rest_low[...]) + dot(first_low, power(0)))
    asked = wanted[...]
    residual = (asked - first) + through
    settled = jnp.sum(residual * residual) <= RESIDUAL * jnp.sum(asked * asked)
    value[...] = residual

    def finish(solved):
        index = lax.broadcasted_iota(jnp.int32, (1, order), 1)
        source = jnp.zeros((1, order), jnp.int32)
        for i, relative in enumerate(PANEL_ORDER):
            source = jnp.where(index // height == i, (me ^ relative) * height, source)
        arrange = (row == source + index % height).astype(f32).astype(bf16)
        high, low = halves(solved * (scale_row * (1.0 / (CODE_TOP * CODE_TOP))))
        high_ref[...] = dot(high, arrange).astype(bf16)
        low_ref[...] = dot(low, arrange).astype(bf16)

    @pl.when(settled)
    def _():
        inverse[0:rows, :] = first

        def correct(index, carry):
            apply(index)
            return carry

        lax.fori_loop(0, count + 1, correct, 0)
        finish(inverse[0:rows, :] + value[...])

    @pl.when(jnp.logical_not(settled))
    def _():
        inverse[...] = entries_ref[...] * scale_col * scale_row

        def pivot(k, carry):
            lanes = lax.broadcasted_iota(jnp.int32, (1, order), 1)
            pivot_row = inverse[pl.ds(k, 1), :]
            head = jnp.sum(jnp.where(lanes == k, pivot_row, 0.0), axis=1, keepdims=True)
            pivot_row = jnp.where(lanes == k, 1.0, pivot_row) / head
            everything = inverse[...]
            column = jnp.sum(jnp.where(col == k, everything, 0.0), axis=1, keepdims=True)
            kept = jnp.where(col == k, 0.0, everything)
            inverse[...] = kept - column * pivot_row
            inverse[pl.ds(k, 1), :] = pivot_row
            return carry

        lax.fori_loop(0, order, pivot, 0)
        whole = entries_ref[...] * scale_col * scale_row
        asked = wanted[...]

        def exact(a, b):
            return jnp.dot(a, b, precision=lax.Precision.HIGHEST, preferred_element_type=f32)

        solved = exact(asked, inverse[...])
        solved = solved + exact(asked - exact(solved, whole), inverse[...])
        finish(solved)


def solve(own, sibling, columns):
    rows, order = columns.shape
    return pl.pallas_call(
        solve_kernel,
        out_shape=(jax.ShapeDtypeStruct((rows, order), bf16),) * 2,
        in_specs=[vmem_spec()] * 3,
        out_specs=(vmem_spec(), vmem_spec()),
        scratch_shapes=[
            VMEM((order, order), f32),
            VMEM((rows, order), f32),
            VMEM((rows, order), f32),
            VMEM(((DOUBLINGS + 1) * order, order), bf16),
            VMEM((order, order), bf16),
            VMEM((order, order), f32),
        ],
        name="solve",
        compiler_params=pltpu.CompilerParams(vmem_limit_bytes=24 * MIB),
    )(own, sibling, columns)


def update_kernel(weights_ref, high_ref, low_ref, *rest):
    panels, out_ref = rest[:-7], rest[-7]
    coefs_high, coefs_low = rest[-6:-4]
    even, odd = rest[-4:-2], rest[-2:]
    step = pl.program_id(0)
    tile = weights_ref.shape[1] // 2
    width = panels[0].shape[1] - 128

    def decode(index, target):
        start = pl.multiple_of(index * tile, tile)
        at = 0
        for ref in panels:
            code = ref[:, pl.ds(start, tile)].astype(jnp.int32).astype(f32)
            high, low = halves(code * jnp.abs(code))
            target[0][at : at + ref.shape[0], :] = high
            target[1][at : at + ref.shape[0], :] = low
            at += ref.shape[0]

    def change(source):
        high = coefs_high[...]
        panel_high = source[0][...]
        return dot(high, panel_high) + (dot(high, source[1][...]) + dot(coefs_low[...], panel_high))

    @pl.when(step == 0)
    def _():
        exponents = jnp.concatenate([ref[:, width:].astype(jnp.int32).astype(f32) for ref in panels], axis=0)
        scale = jnp.exp2(jnp.transpose(exponents)[0:1, :] * 0.125)
        high, low = halves((high_ref[...].astype(f32) + low_ref[...].astype(f32)) * scale)
        coefs_high[...] = high
        coefs_low[...] = low
        decode(0, even)

    decode(2 * step + 1, odd)
    out_ref[:, 0:tile] = (weights_ref[:, 0:tile].astype(f32) - change(even)).astype(bf16)
    decode(jnp.minimum(2 * step + 2, width // tile - 1), even)
    out_ref[:, tile:] = (weights_ref[:, tile:].astype(f32) - change(odd)).astype(bf16)


def update(weights, high, low, panels):
    rows, width = weights.shape
    order = high.shape[1]
    return pl.pallas_call(
        update_kernel,
        out_shape=jax.ShapeDtypeStruct((rows, width), bf16),
        grid=(width // (2 * TILE),),
        in_specs=[
            pl.BlockSpec((rows, 2 * TILE), lambda i: (0, i)),
            pl.BlockSpec((rows, order), lambda i: (0, 0)),
            pl.BlockSpec((rows, order), lambda i: (0, 0)),
        ]
        + [vmem_spec()] * len(panels),
        out_specs=pl.BlockSpec((rows, 2 * TILE), lambda i: (0, i)),
        scratch_shapes=[VMEM((rows, order), bf16)] * 2 + [VMEM((order, TILE), bf16)] * 4,
        name="update",
        compiler_params=pltpu.CompilerParams(vmem_limit_bytes=24 * MIB),
    )(weights, high, low, *panels)


def swap(value, axis, relative):
    size = lax.axis_size(axis)
    return lax.ppermute(value, axis, [(i, i ^ relative) for i in range(size)])


def grow(value, axis, relative):
    return join(value, swap(value, axis, relative))


def join(*values):
    return lax.optimization_barrier(jnp.concatenate(values, axis=0))


def prune(weights, panel_first, panel_second, removed_first, removed_second):
    rows = weights.shape[0]
    height = 2 * panel_first.shape[0]
    order = height * lax.axis_size("row")
    chosen_first = removed_first[None, :]
    chosen_second = removed_second[None, :]
    codes, slots, mine = prepare(panel_first, panel_second, chosen_first, chosen_second, weights)

    near = grow(grow(slots, "col", Z_HALF), "col", X_ONE)
    far = swap(near, "col", X_THREE)
    entries, places = compact(near, far, height, order)
    entries = grow(entries, "row", Z_ONE)
    entries = grow(entries, "row", Z_TWO)
    entries = grow(entries, "row", Y_ONE)
    entries = grow(entries, "row", Y_THREE)
    sibling = swap(entries, "row", CORE)

    mine_near = grow(grow(mine, "col", Z_HALF), "col", X_ONE)
    mine_far = swap(mine_near, "col", X_THREE)
    columns = place(mine_near, mine_far, places, rows, order)

    even = grow(codes, "row", Z_ONE)
    even_one = swap(even, "row", Y_ONE)
    even_three = swap(even, "row", Y_THREE)
    even_two = swap(even_one, "row", Y_THREE)
    odd = join(swap(codes, "row", Z_TWO), swap(codes, "row", Z_THREE))
    odd_three = swap(odd, "row", Y_THREE)
    odd_one = swap(odd, "row", Y_ONE)
    odd_two = swap(odd_three, "row", Y_ONE)
    panels = [even, even_one, even_three, even_two, odd, odd_three, odd_one, odd_two]
    panels = panels + [swap(p, "row", CORE) for p in panels]

    high, low = solve(entries, sibling, columns)
    return update(weights, high, low, panels)


def solution(mesh):
    return jax.shard_map(
        prune,
        mesh=mesh,
        in_specs=(P("row", "col"), P("row", "col"), P("row", "col"), P("col"), P("col")),
        out_specs=P("row", "col"),
        check_vma=False,
    )
```

```python
import jax
import jax.numpy as jnp
from jax import lax
from jax.experimental import pallas as pl
from jax.experimental.pallas import tpu as pltpu
from jax.sharding import PartitionSpec as P


f32 = jnp.float32
bf16 = jnp.bfloat16
VMEM = pltpu.VMEM
MIB = 1 << 20
TOLERANCE = 3e-5
DOUBLINGS = 6
RESIDUAL = 1e-5
CODE_TOP = 32767.0
PARTS = 4
TILE = 512
CORE, Y_ONE, Y_THREE, Z_ONE, Z_TWO, Z_THREE = 1, 2, 6, 8, 16, 24
X_ONE, X_THREE, Z_HALF = 1, 3, 4
OWNER_ORDER = (0, 4, 1, 5, 3, 7, 2, 6)
ENTRY_ORDER = tuple(c + y * 2 + z * 8 for c in (0, 1) for y in (0, 1, 3, 2) for z in range(4))
PANEL_ORDER = tuple(
    c + y * 2 + z * 8
    for c in (0, 1)
    for ys, zs in (((0, 1, 3, 2), (0, 1)), ((0, 3, 1, 2), (2, 3)))
    for y in ys
    for z in zs
)


def vmem_spec():
    return pl.BlockSpec(memory_space=VMEM)


def halves(value):
    high = value.astype(bf16)
    low = (value - high.astype(f32)).astype(bf16)
    return high, low


def dot(a, b):
    return jnp.dot(a, b, preferred_element_type=f32)


def code_scale(exponent):
    return jnp.exp2(exponent.astype(f32) * 0.125)


def prepare_kernel(
    first_hbm,
    second_hbm,
    chosen_first_hbm,
    chosen_second_hbm,
    weights_hbm,
    codes_ref,
    slots_ref,
    mine_ref,
    panels_ref,
    chosen_first_ref,
    chosen_second_ref,
    weights_ref,
    onehot_ref,
    arrived,
):
    half, width = first_hbm.shape
    height = 2 * half
    part = width // PARTS
    moves = [
        (chosen_first_hbm, chosen_first_ref),
        (chosen_second_hbm, chosen_second_ref),
        (first_hbm, panels_ref.at[0:half]),
        (second_hbm, panels_ref.at[half:height]),
    ]
    for i in range(PARTS):
        columns = pl.ds(i * part, part)
        moves.append((weights_hbm.at[:, columns], weights_ref.at[:, columns]))
    copies = [
        pltpu.make_async_copy(source, target, arrived.at[i])
        for i, (source, target) in enumerate(moves)
    ]
    for copy in copies:
        copy.start()
    for copy in copies[0:4]:
        copy.wait()
    panels = panels_ref[...]
    size = jnp.abs(panels)
    most = jnp.maximum(jnp.max(size, axis=1, keepdims=True), 1e-30)
    exponent = jnp.ceil(jnp.log2(most) * 8.0).astype(jnp.int32)
    root = jnp.sqrt(size / code_scale(exponent))
    level = jnp.minimum(root * CODE_TOP + 0.5, CODE_TOP).astype(jnp.int32)
    codes_ref[:, 0:width] = jnp.where(panels < 0, -level, level).astype(jnp.int16)
    codes_ref[:, width:] = jnp.broadcast_to(exponent, (height, 128)).astype(jnp.int16)

    chosen = jnp.concatenate([chosen_first_ref[...], chosen_second_ref[...]], axis=1)
    column = lax.broadcasted_iota(jnp.int32, (width, chosen.shape[1]), 0)
    onehot_ref[...] = (column == chosen).astype(f32).astype(bf16)
    high = panels.astype(bf16)
    rest = panels - high.astype(f32)
    middle = rest.astype(bf16)
    low = (rest - middle.astype(f32)).astype(bf16)
    pieces = dot(jnp.concatenate([high, middle, low], axis=0), onehot_ref[...])
    slots_ref[0 : 3 * height, :] = pieces.astype(bf16)
    live = jnp.broadcast_to((chosen >= 0).astype(f32), (height, chosen.shape[1]))
    slots_ref[3 * height :, :] = live.astype(bf16)

    taken = None
    for i, copy in enumerate(copies[4:]):
        copy.wait()
        at = i * part
        share = dot(weights_ref[:, at : at + part], onehot_ref[at : at + part, :])
        taken = share if taken is None else taken + share
    mine_ref[...] = taken.astype(bf16)


def prepare(first, second, chosen_first, chosen_second, weights):
    height, width = 2 * first.shape[0], first.shape[1]
    rows = weights.shape[0]
    slots = 2 * chosen_first.shape[1]
    return pl.pallas_call(
        prepare_kernel,
        out_shape=(
            jax.ShapeDtypeStruct((height, width + 128), jnp.int16),
            jax.ShapeDtypeStruct((4 * height, slots), bf16),
            jax.ShapeDtypeStruct((rows, slots), bf16),
        ),
        in_specs=[pl.BlockSpec(memory_space=pltpu.HBM)] * 5,
        out_specs=(vmem_spec(),) * 3,
        scratch_shapes=[
            VMEM((height, width), f32),
            VMEM(chosen_first.shape, jnp.int32),
            VMEM(chosen_second.shape, jnp.int32),
            VMEM((rows, width), bf16),
            VMEM((width, slots), bf16),
            pltpu.SemaphoreType.DMA((4 + PARTS,)),
        ],
        name="prepare",
        compiler_params=pltpu.CompilerParams(vmem_limit_bytes=56360960),
    )(first, second, chosen_first, chosen_second, weights)


def mover(place, order):
    target = lax.broadcasted_iota(jnp.int32, (order, place.shape[1]), 0)
    return (target == place).astype(f32).astype(bf16)


def against(a, b):
    return lax.dot_general(a, b, (((1,), (1,)), ((), ())), preferred_element_type=f32)


def compact_kernel(near_ref, far_ref, entries_ref, places_ref):
    height, order = entries_ref.shape
    slots = near_ref.shape[1]
    half = slots // 2
    total = 4 * height
    per_device = height // 2
    me = lax.axis_index("col")
    lane = lax.broadcasted_iota(jnp.int32, (1, slots), 1)
    in_second = lane >= half
    slot = jnp.where(in_second, lane - half, lane)
    group = near_ref.shape[0] // total

    def block(index, start, stop):
        ref = near_ref if index < group else far_ref
        at = (index % group) * total
        return ref[at + start : at + stop, :]

    live = [block(i, 3 * height, total).astype(f32)[0:1, :] for i in range(len(OWNER_ORDER))]
    firsts = [jnp.sum(jnp.where(in_second, 0.0, x), axis=1, keepdims=True) for x in live]
    seconds = [jnp.sum(jnp.where(in_second, x, 0.0), axis=1, keepdims=True) for x in live]
    result = None
    for i, relative in enumerate(OWNER_ORDER):
        base_first = jnp.zeros((1, 1), f32)
        base_second = jnp.zeros((1, 1), f32)
        for j, other in enumerate(OWNER_ORDER):
            before = ((me ^ other) < (me ^ relative)).astype(f32)
            base_first = base_first + before * firsts[j]
            base_second = base_second + before * seconds[j]
        position = jnp.where(in_second, base_second, base_first).astype(jnp.int32) + slot
        place = (
            (position // per_device) * height
            + jnp.where(in_second, per_device, 0)
            + position % per_device
        )
        place = jnp.where(live[i] > 0.5, place, -1)
        places_ref[i : i + 1, :] = place
        share = against(block(i, 0, 3 * height), mover(place, order))
        result = share if result is None else result + share
    high = result[0:height, :]
    middle = result[height : 2 * height, :]
    entries_ref[...] = high + (middle + result[2 * height : 3 * height, :])


def compact(near, far, height, order):
    return pl.pallas_call(
        compact_kernel,
        out_shape=(
            jax.ShapeDtypeStruct((height, order), f32),
            jax.ShapeDtypeStruct((len(OWNER_ORDER), near.shape[1]), jnp.int32),
        ),
        in_specs=[vmem_spec()] * 2,
        out_specs=(vmem_spec(), vmem_spec()),
        name="compact",
        compiler_params=pltpu.CompilerParams(vmem_limit_bytes=8 * MIB),
    )(near, far)


def place_kernel(near_ref, far_ref, places_ref, columns_ref):
    rows, order = columns_ref.shape
    group = near_ref.shape[0] // rows
    result = None
    for i in range(len(OWNER_ORDER)):
        ref = near_ref if i < group else far_ref
        at = (i % group) * rows
        share = against(ref[at : at + rows, :], mover(places_ref[i : i + 1, :], order))
        result = share if result is None else result + share
    columns_ref[...] = result.astype(bf16)


def place(near, far, places, rows, order):
    return pl.pallas_call(
        place_kernel,
        out_shape=jax.ShapeDtypeStruct((rows, order), bf16),
        in_specs=[vmem_spec()] * 3,
        out_specs=vmem_spec(),
        name="place",
        compiler_params=pltpu.CompilerParams(vmem_limit_bytes=8 * MIB),
    )(near, far, places)


def solve_kernel(*refs):
    parts = refs[:-9]
    columns_ref, high_ref, low_ref, entries_ref, value, wanted, powers, rest_low, inverse = refs[-9:]
    order = entries_ref.shape[0]
    rows = columns_ref.shape[0]
    me = lax.axis_index("row")
    height = order // len(ENTRY_ORDER)
    share = len(ENTRY_ORDER) // len(parts)
    for i, relative in enumerate(ENTRY_ORDER):
        ref = parts[i // share]
        at = (i % share) * height
        start = pl.multiple_of((me ^ relative) * height, height)
        entries_ref[pl.ds(start, height), :] = ref[at : at + height, :]
    row = lax.broadcasted_iota(jnp.int32, (order, order), 0)
    col = lax.broadcasted_iota(jnp.int32, (order, order), 1)
    entries = entries_ref[...]
    diagonal = jnp.where(row == col, entries, 0.0)
    scale_row = lax.rsqrt(jnp.sum(diagonal, axis=0, keepdims=True))
    scale_col = lax.rsqrt(jnp.sum(diagonal, axis=1, keepdims=True))
    unit = entries * scale_col * scale_row
    rest = jnp.where(row == col, 1.0 - unit, -unit)
    rest_high = rest.astype(bf16)
    powers[0:order, :] = rest_high
    rest_low[...] = (rest - rest_high.astype(f32)).astype(bf16)
    scaled = columns_ref[...].astype(f32) * scale_row
    wanted[...] = scaled
    value[...] = scaled

    def power(index):
        return powers[pl.ds(pl.multiple_of(index * order, order), order), :]

    def apply(index):
        value[...] += dot(value[...].astype(bf16), power(index))

    def going(state):
        count, left = state
        return jnp.logical_and(count < DOUBLINGS, jnp.logical_not(left < TOLERANCE))

    def double(state):
        count, _ = state
        this = power(count)
        apply(count)
        squared = dot(this, this)
        powers[pl.ds(pl.multiple_of((count + 1) * order, order), order), :] = squared.astype(bf16)
        return count + 1, jnp.sum(squared * squared)

    count, _ = lax.while_loop(going, double, (jnp.int32(0), jnp.sum(rest * rest)))
    apply(count)
    first = value[...]
    first_high, first_low = halves(first)
    through = dot(first_high, power(0)) + (dot(first_high, rest_low[...]) + dot(first_low, power(0)))
    asked = wanted[...]
    residual = (asked - first) + through
    settled = jnp.sum(residual * residual) <= RESIDUAL * jnp.sum(asked * asked)
    value[...] = residual

    def finish(solved):
        index = lax.broadcasted_iota(jnp.int32, (1, order), 1)
        source = jnp.zeros((1, order), jnp.int32)
        for i, relative in enumerate(PANEL_ORDER):
            source = jnp.where(index // height == i, (me ^ relative) * height, source)
        arrange = (row == source + index % height).astype(f32).astype(bf16)
        high, low = halves(solved * (scale_row * (1.0 / (CODE_TOP * CODE_TOP))))
        high_ref[...] = dot(high, arrange).astype(bf16)
        low_ref[...] = dot(low, arrange).astype(bf16)

    @pl.when(settled)
    def _():
        inverse[0:rows, :] = first

        def correct(index, carry):
            apply(index)
            return carry

        lax.fori_loop(0, count + 1, correct, 0)
        finish(inverse[0:rows, :] + value[...])

    @pl.when(jnp.logical_not(settled))
    def _():
        inverse[...] = entries_ref[...] * scale_col * scale_row

        def pivot(k, carry):
            lanes = lax.broadcasted_iota(jnp.int32, (1, order), 1)
            pivot_row = inverse[pl.ds(k, 1), :]
            head = jnp.sum(jnp.where(lanes == k, pivot_row, 0.0), axis=1, keepdims=True)
            pivot_row = jnp.where(lanes == k, 1.0, pivot_row) / head
            everything = inverse[...]
            column = jnp.sum(jnp.where(col == k, everything, 0.0), axis=1, keepdims=True)
            kept = jnp.where(col == k, 0.0, everything)
            inverse[...] = kept - column * pivot_row
            inverse[pl.ds(k, 1), :] = pivot_row
            return carry

        lax.fori_loop(0, order, pivot, 0)
        whole = entries_ref[...] * scale_col * scale_row
        asked = wanted[...]

        def exact(a, b):
            return jnp.dot(a, b, precision=lax.Precision.HIGHEST, preferred_element_type=f32)

        solved = exact(asked, inverse[...])
        solved = solved + exact(asked - exact(solved, whole), inverse[...])
        finish(solved)


def solve(parts, columns):
    rows, order = columns.shape
    return pl.pallas_call(
        solve_kernel,
        out_shape=(jax.ShapeDtypeStruct((rows, order), bf16),) * 2,
        in_specs=[vmem_spec()] * (len(parts) + 1),
        out_specs=(vmem_spec(), vmem_spec()),
        scratch_shapes=[
            VMEM((order, order), f32),
            VMEM((rows, order), f32),
            VMEM((rows, order), f32),
            VMEM(((DOUBLINGS + 1) * order, order), bf16),
            VMEM((order, order), bf16),
            VMEM((order, order), f32),
        ],
        name="solve",
        compiler_params=pltpu.CompilerParams(vmem_limit_bytes=24 * MIB),
    )(*parts, columns)


def update_kernel(weights_ref, high_ref, low_ref, *rest):
    panels, out_ref = rest[:-7], rest[-7]
    coefs_high, coefs_low = rest[-6:-4]
    even, odd = rest[-4:-2], rest[-2:]
    step = pl.program_id(0)
    tile = weights_ref.shape[1] // 2
    width = panels[0].shape[1] - 128

    def decode(index, target):
        start = pl.multiple_of(index * tile, tile)
        at = 0
        for ref in panels:
            code = ref[:, pl.ds(start, tile)].astype(jnp.int32).astype(f32)
            high, low = halves(code * jnp.abs(code))
            target[0][at : at + ref.shape[0], :] = high
            target[1][at : at + ref.shape[0], :] = low
            at += ref.shape[0]

    def change(source):
        high = coefs_high[...]
        panel_high = source[0][...]
        return dot(high, panel_high) + (dot(high, source[1][...]) + dot(coefs_low[...], panel_high))

    @pl.when(step == 0)
    def _():
        exponents = jnp.concatenate([ref[:, width:].astype(jnp.int32).astype(f32) for ref in panels], axis=0)
        scale = jnp.exp2(jnp.transpose(exponents)[0:1, :] * 0.125)
        high, low = halves((high_ref[...].astype(f32) + low_ref[...].astype(f32)) * scale)
        coefs_high[...] = high
        coefs_low[...] = low
        decode(0, even)

    decode(2 * step + 1, odd)
    out_ref[:, 0:tile] = (weights_ref[:, 0:tile].astype(f32) - change(even)).astype(bf16)
    decode(jnp.minimum(2 * step + 2, width // tile - 1), even)
    out_ref[:, tile:] = (weights_ref[:, tile:].astype(f32) - change(odd)).astype(bf16)


def update(weights, high, low, panels):
    rows, width = weights.shape
    order = high.shape[1]
    return pl.pallas_call(
        update_kernel,
        out_shape=jax.ShapeDtypeStruct((rows, width), bf16),
        grid=(width // (2 * TILE),),
        in_specs=[
            pl.BlockSpec((rows, 2 * TILE), lambda i: (0, i)),
            pl.BlockSpec((rows, order), lambda i: (0, 0)),
            pl.BlockSpec((rows, order), lambda i: (0, 0)),
        ]
        + [vmem_spec()] * len(panels),
        out_specs=pl.BlockSpec((rows, 2 * TILE), lambda i: (0, i)),
        scratch_shapes=[VMEM((rows, order), bf16)] * 2 + [VMEM((order, TILE), bf16)] * 4,
        name="update",
        compiler_params=pltpu.CompilerParams(vmem_limit_bytes=24 * MIB),
    )(weights, high, low, *panels)


def swap(value, axis, relative):
    size = lax.axis_size(axis)
    return lax.ppermute(value, axis, [(i, i ^ relative) for i in range(size)])


def grow(value, axis, relative):
    return join(value, swap(value, axis, relative))


def join(*values):
    return lax.optimization_barrier(jnp.concatenate(values, axis=0))


def prune(weights, panel_first, panel_second, removed_first, removed_second):
    rows = weights.shape[0]
    height = 2 * panel_first.shape[0]
    order = height * lax.axis_size("row")
    chosen_first = removed_first[None, :]
    chosen_second = removed_second[None, :]
    codes, slots, mine = prepare(panel_first, panel_second, chosen_first, chosen_second, weights)

    near = grow(grow(slots, "col", Z_HALF), "col", X_ONE)
    far = swap(near, "col", X_THREE)
    entries, places = compact(near, far, height, order)
    entries = grow(entries, "row", Z_ONE)
    entries = grow(entries, "row", Z_TWO)
    entries_one = swap(entries, "row", Y_ONE)
    entries_three = swap(entries, "row", Y_THREE)
    entries_two = swap(entries_one, "row", Y_THREE)
    parts = [entries, entries_one, entries_three, entries_two]
    parts = parts + [swap(e, "row", CORE) for e in parts]

    mine_near = grow(grow(mine, "col", Z_HALF), "col", X_ONE)
    mine_far = swap(mine_near, "col", X_THREE)
    columns = place(mine_near, mine_far, places, rows, order)

    even = grow(codes, "row", Z_ONE)
    even_one = swap(even, "row", Y_ONE)
    even_three = swap(even, "row", Y_THREE)
    even_two = swap(even_one, "row", Y_THREE)
    odd = join(swap(codes, "row", Z_TWO), swap(codes, "row", Z_THREE))
    odd_three = swap(odd, "row", Y_THREE)
    odd_one = swap(odd, "row", Y_ONE)
    odd_two = swap(odd_three, "row", Y_ONE)
    panels = [even, even_one, even_three, even_two, odd, odd_three, odd_one, odd_two]
    panels = panels + [swap(p, "row", CORE) for p in panels]

    high, low = solve(parts, columns)
    return update(weights, high, low, panels)


def solution(mesh):
    return jax.shard_map(
        prune,
        mesh=mesh,
        in_specs=(P("row", "col"), P("row", "col"), P("row", "col"), P("col"), P("col")),
        out_specs=P("row", "col"),
        check_vma=False,
    )
```
